128 devices in a mesh: seq: 32 (over x, y, core), tp: 4 (over z).
Axes of the slice: x: 4, y: 4, z: 4, core: 2. Of those that a mesh axis runs over, the one named last changes fastest.
Arguments:
- tokens: bfloat16 [49152, 1792], P('seq', 'tp'), may hold values from -8 to 8
- w_query: bfloat16 [1792, 256], P('seq', 'tp'), may hold values from -0.125 to 0.125
- w_key: bfloat16 [1792, 256], P('seq', 'tp'), may hold values from -0.125 to 0.125
- w_value: bfloat16 [1792, 1792], P('seq', 'tp'), may hold values from -0.125 to 0.125
- prompt_lengths: int32 [32], replicated, may hold values from 1 to 24576, as said below
- owner_slot: int32 [32], replicated, may hold values from 0 to 31, each once
- resume_flag: int32 [32], replicated, may hold values 0 or 1
- init_state: float32 [32, 273, 1792], P('seq', None, 'tp'), may hold values from -0.5 to 0.5
- init_norm: float32 [32, 273, 16], P('seq', None, 'tp'), may hold values from -0.5 to 0.5, as said below
Outputs:
- heads_out: bfloat16 [49152, 1792], P('seq', 'tp')
- final_state: float32 [32, 273, 1792], P('seq', None, 'tp')
- final_norm: float32 [32, 273, 16], P('seq', None, 'tp')
The draws below stay inside these ranges and needn't reach their ends.
Inputs may be any that keep to these rules, and one draw needn't show every extreme that they name: `prompt_lengths`: prompt r takes the packed positions after those of prompts 0 to r - 1; the lengths sum to 49152; the longest prompt starts and ends at multiples of 1536; every block of 1536 positions that it does not cover holds the end of at least one prompt; no block holds the ends of more than 4 prompts, and one holds exactly 4. `owner_slot`: every row of the state arrays belongs to exactly one request. `resume_flag`: 1 where the request continues from its given states, 0 where it is new. `init_norm`: for every request and head, the inner product with phi(u) is at least half of the row's first entry, and that entry is positive, for every u.
All inputs are finite; a program needn't handle non-finite values.
Results may differ from the reference program's by a relative error of at most 0.0041.
Values may be sent and summed in bfloat16 or wider, within the bound.
A program may use at most 192 MiB of HBM per device.

```python
import math
import jax
import jax.numpy as jnp
from jax import lax

D = 1792
HEADS = 16
FD = 16
HV = 112
TOK_DEV = 1536
END_SLOTS = 4
FEAT = 273
TOKENS = 49152
REQS = 32
MAXLEN = 24576


def draw_tokens(key, part):
    noise_key = jax.random.fold_in(key, 31)
    mean_key = jax.random.fold_in(key, 32)
    block_total = TOKENS // TOK_DEV
    noise = jnp.clip(jax.random.normal(noise_key, (block_total, TOK_DEV, D), jnp.float32), -5.0, 5.0)
    means = 0.7 * jnp.clip(jax.random.normal(mean_key, (block_total, 1, D), jnp.float32), -4.0, 4.0)
    return jnp.clip(noise + means, -8.0, 8.0).reshape(TOKENS, D).astype(jnp.bfloat16)


def draw_prompt_lengths(key, part):
    block_total = TOKENS // TOK_DEV
    long_blocks = MAXLEN // TOK_DEV
    short_blocks = block_total - long_blocks
    place_key = jax.random.fold_in(key, 5)
    shuffle_key = jax.random.fold_in(key, 6)
    spot_key = jax.random.fold_in(key, 7)
    long_first = jax.random.randint(place_key, (), 0, short_blocks + 1)
    shuffled = jax.random.permutation(shuffle_key, jnp.arange(short_blocks, dtype=jnp.int32))
    rank_of = jnp.zeros((short_blocks,), jnp.int32).at[shuffled].set(jnp.arange(short_blocks, dtype=jnp.int32))
    short_ends = jnp.where(rank_of == 0, END_SLOTS, jnp.where(rank_of <= short_blocks - END_SLOTS, 2, 1)).astype(jnp.int32)
    blocks = jnp.arange(block_total, dtype=jnp.int32)
    in_long = (blocks >= long_first) & (blocks < long_first + long_blocks)
    long_last = blocks == long_first + long_blocks - 1
    short_index = jnp.clip(jnp.where(blocks < long_first, blocks, blocks - long_blocks), 0, short_blocks - 1)
    counts = jnp.where(in_long, long_last.astype(jnp.int32), short_ends[short_index])
    forced = long_last | (blocks == long_first - 1) | (blocks == block_total - 1)
    offsets = jnp.arange(TOK_DEV, dtype=jnp.int32)
    spread_max = 2 ** 30 // TOK_DEV
    scores = jax.random.randint(spot_key, (block_total, TOK_DEV), 0, spread_max, dtype=jnp.int32) * TOK_DEV + offsets[None, :]
    scores = jnp.where(forced[:, None] & (offsets[None, :] == TOK_DEV - 1), 2 ** 30 + offsets[None, :], scores)
    top_values, top_spots = lax.top_k(scores, END_SLOTS)
    kept = (jnp.arange(END_SLOTS, dtype=jnp.int32)[None, :] < counts[:, None]).astype(jnp.int32)
    end_spots = blocks[:, None] * TOK_DEV + top_spots + 1
    end_mask = jnp.zeros((TOKENS + 1,), jnp.int32).at[end_spots.reshape(-1)].add(kept.reshape(-1))
    ranked = end_mask[1:] * (TOKENS + 1 - jnp.arange(1, TOKENS + 1, dtype=jnp.int32))
    best_values, best_spots = lax.top_k(ranked, REQS)
    end_points = TOKENS + 1 - best_values
    return (end_points - jnp.concatenate([jnp.zeros((1,), jnp.int32), end_points[:-1]])).astype(jnp.int32)


def past_terms(key):
    base_key = jax.random.fold_in(key, 11)
    count_key = jax.random.fold_in(base_key, 1)
    mean_key = jax.random.fold_in(base_key, 2)
    diag_key = jax.random.fold_in(base_key, 3)
    counts = jnp.exp(jax.random.uniform(count_key, (REQS,), jnp.float32, math.log(1.0 / 64.0), math.log(0.5)))
    key_means = jnp.clip(0.5 * jax.random.normal(mean_key, (REQS, HEADS, FD), jnp.float32), -1.0, 1.0)
    diagonal = jax.random.uniform(diag_key, (REQS, HEADS, FD), jnp.float32, 0.5, 1.5)
    return (counts, key_means, diagonal)


def draw_init_norm(key, part):
    counts, key_means, diagonal = past_terms(key)
    second = key_means[..., :, None] * key_means[..., None, :] + diagonal[..., :, None] * jnp.eye(FD, dtype=jnp.float32)
    second = second.reshape(REQS, HEADS, FD * FD) / math.sqrt(2.0 * FD)
    unit_column = jnp.ones((REQS, HEADS, 1), jnp.float32)
    feature_rows = jnp.concatenate([unit_column, key_means / FD ** 0.25, second], axis=-1)
    return jnp.transpose(feature_rows * counts[:, None, None], (0, 2, 1))


def draw_init_state(key, part):
    counts, key_means, diagonal = past_terms(key)
    noise_key = jax.random.fold_in(key, 23)
    noise_part = 0.2 * jnp.clip(jax.random.normal(noise_key, (REQS, FEAT, HEADS * HV), jnp.float32), -4.0, 4.0)
    return noise_part * counts[:, None, None]


def plant(array, rng, smallest, largest):
    place = [jax.random.randint(jax.random.fold_in(rng, axis), (), 0, length) for axis, length in enumerate(array.shape)]
    main_axis = array.shape.index(max(array.shape))
    beside = place[:main_axis] + [(place[main_axis] + 1) % array.shape[main_axis]] + place[main_axis + 1:]
    return array.at[tuple(place)].set(smallest).at[tuple(beside)].set(largest)


def block_scale(stream_key, extent, cuts, least, top_value):
    def one(position, shards_of):
        draws = jax.random.uniform(jax.random.fold_in(jax.random.fold_in(stream_key, 6), position), (shards_of,), jnp.float32, least / len(cuts), top_value / len(cuts))
        return jnp.repeat(jnp.exp(draws), extent[position] // shards_of).reshape((-1,) + (1,) * (len(extent) - position - 1))

    factor_of = one(*cuts[0])
    for cut in cuts[1:]:
        factor_of = factor_of * one(*cut)
    return factor_of


def gaussian(key, extent, spread, most, split=(), held_as=jnp.bfloat16):
    array = jax.random.normal(key, extent, jnp.float32) * spread
    if len(split) > 0:
        array = block_scale(key, extent, split, -0.22, 0.18) * array
    return jnp.clip(array, min=-most, max=most).astype(held_as)


def setup_inputs(seed: int = 0) -> dict:
    keys = jax.random.split(jax.random.key(seed), 10)
    return {
        "tokens": draw_tokens(jax.random.fold_in(keys[9], 71), 0),
        "w_query": gaussian(keys[1], (D, HEADS * FD), D ** -0.5, 0.125, ((0, 32), (1, 4))),
        "w_key": gaussian(keys[2], (D, HEADS * FD), D ** -0.5, 0.125, ((0, 32), (1, 4))),
        "w_value": gaussian(keys[3], (D, HEADS * HV), D ** -0.5, 0.125, ((0, 32), (1, 4))),
        "prompt_lengths": draw_prompt_lengths(jax.random.fold_in(keys[9], 71), 0),
        "owner_slot": jax.random.permutation(keys[5], REQS).astype(jnp.int32),
        "resume_flag": plant((jax.random.randint(keys[6], (REQS,), 0, 3) < 2).astype(jnp.int32), jax.random.fold_in(keys[6], 1), 0, 1),
        "init_state": draw_init_state(jax.random.fold_in(keys[9], 71), 0),
        "init_norm": draw_init_norm(jax.random.fold_in(keys[9], 71), 0),
    }


full_precision = lax.Precision.HIGHEST

def feature_map(vectors):
    feat_dim = vectors.shape[-1]
    second = (vectors[..., :, None] * vectors[..., None, :]).reshape(vectors.shape[:-1] + (feat_dim * feat_dim,))
    unit_column = jnp.ones(vectors.shape[:-1] + (1,), vectors.dtype)
    return jnp.concatenate([unit_column, vectors / feat_dim ** 0.25, second / math.sqrt(2.0 * feat_dim)], axis=-1)

def reference(tokens, w_query, w_key, w_value, prompt_lengths, owner_slot, resume_flag, init_state, init_norm):
    scale_state = 1.0 / MAXLEN
    query_proj = jnp.dot(tokens, w_query, preferred_element_type=jnp.float32).astype(jnp.bfloat16)
    key_proj = jnp.dot(tokens, w_key, preferred_element_type=jnp.float32).astype(jnp.bfloat16)
    value_proj = jnp.dot(tokens, w_value, preferred_element_type=jnp.float32).astype(jnp.bfloat16)
    end_offsets = jnp.cumsum(prompt_lengths).astype(jnp.int32)
    positions = jnp.arange(TOKENS, dtype=jnp.int32)
    request_ids = lax.optimization_barrier(jnp.sum((end_offsets[None, :] <= positions[:, None]).astype(jnp.int32), axis=1)).astype(jnp.int32)
    resume_weight = resume_flag.astype(jnp.float32)
    start_state = resume_weight[:, None, None] * init_state[owner_slot]
    start_norm = resume_weight[:, None, None] * init_norm[owner_slot]
    block_count = TOKENS // TOK_DEV
    block_inputs = (query_proj.reshape(block_count, TOK_DEV, HEADS, FD), key_proj.reshape(block_count, TOK_DEV, HEADS, FD), value_proj.reshape(block_count, TOK_DEV, HEADS, HV), request_ids.reshape(block_count, TOK_DEV), positions.reshape(block_count, TOK_DEV))

    def block_step(running, inputs):
        run_state, run_norm = running
        block_q, block_k, block_v, block_req, block_pos = inputs

        def one_head(head_inputs):
            head_q, head_k, head_v = head_inputs
            scores = lax.dot_general(head_q, head_k, (((1,), (1,)), ((), ())), preferred_element_type=jnp.float32) / math.sqrt(FD)
            allowed = (block_pos[None, :] <= block_pos[:, None]) & (block_req[None, :] == block_req[:, None])
            weight = jnp.where(allowed, 1.0 + scores + 0.5 * scores * scores, 0.0).astype(jnp.bfloat16)
            return (jnp.dot(weight, head_v, preferred_element_type=jnp.float32), lax.optimization_barrier(jnp.sum(weight.astype(jnp.float32), axis=1)))
        local_num, local_den = lax.map(one_head, (jnp.moveaxis(block_q, 1, 0), jnp.moveaxis(block_k, 1, 0), jnp.moveaxis(block_v, 1, 0)))
        phi_q = feature_map(block_q.astype(jnp.float32))
        phi_k = feature_map(block_k.astype(jnp.float32))
        value_f = block_v.astype(jnp.float32)

        def per_request(req, totals):
            prior_num, prior_den, state_all, norm_all = totals
            chosen = (block_req == req).astype(jnp.float32)
            req_state = lax.dynamic_index_in_dim(state_all, req, 0, keepdims=False).reshape(FEAT, HEADS, HV)
            req_norm = lax.dynamic_index_in_dim(norm_all, req, 0, keepdims=False)
            prior_num = prior_num + chosen[:, None, None] * jnp.einsum('thf,fhj->thj', phi_q, req_state, precision=full_precision)
            prior_den = prior_den + chosen[:, None] * jnp.einsum('thf,fh->th', phi_q, req_norm, precision=full_precision)
            weighted = phi_k * chosen[:, None, None]
            new_state = req_state + scale_state * jnp.einsum('thf,thj->fhj', weighted, value_f, precision=full_precision)
            new_norm = req_norm + scale_state * lax.optimization_barrier(jnp.sum(weighted, axis=0)).T
            state_all = lax.dynamic_update_index_in_dim(state_all, new_state.reshape(FEAT, HEADS * HV), req, 0)
            norm_all = lax.dynamic_update_index_in_dim(norm_all, new_norm, req, 0)
            return (prior_num, prior_den, state_all, norm_all)
        start = (jnp.zeros((TOK_DEV, HEADS, HV), jnp.float32), jnp.zeros((TOK_DEV, HEADS), jnp.float32), run_state, run_norm)
        prior_num, prior_den, run_state, run_norm = lax.fori_loop(block_req[0], block_req[-1] + 1, per_request, start)
        numer = prior_num + scale_state * jnp.moveaxis(local_num, 0, 1)
        denom = prior_den + scale_state * local_den.T
        block_out = (numer / denom[:, :, None]).reshape(TOK_DEV, HEADS * HV).astype(jnp.bfloat16)
        return ((run_state, run_norm), block_out)
    (run_state, run_norm), all_out = lax.scan(block_step, (start_state, start_norm), block_inputs)
    heads_out = all_out.reshape(TOKENS, HEADS * HV)
    final_state = jnp.zeros_like(run_state).at[owner_slot].set(run_state)
    final_norm = jnp.zeros_like(run_norm).at[owner_slot].set(run_norm)
    return (heads_out, final_state, final_norm)
```

```python
import functools
import math

import jax
import jax.numpy as jnp
import numpy as np
from jax import lax
from jax.experimental import pallas as pl
from jax.experimental.pallas import tpu as pltpu
from jax.sharding import PartitionSpec as P

FD = 16
HD = 4
HV = 112
FEAT = 273
ENDS = 4
SLOTS = 5
ROWS = 192
MESH = pl.DeviceIdType.MESH
F32 = jnp.float32
BF16 = jnp.bfloat16


def tables(norm):
    e1 = np.zeros((FD, 256), np.float32)
    e2 = np.zeros((FD, 256), np.float32)
    b1 = np.zeros((256,), np.float32)
    b2 = np.zeros((256,), np.float32)
    coef = np.zeros((256,), np.float32)
    fold = np.zeros((ROWS, FEAT), np.float32)
    fold_scale = np.zeros((ROWS, 1), np.float32)
    spread = np.zeros((FEAT, ROWS), np.float32)
    spread_scale = np.zeros((FEAT, 1), np.float32)
    root = math.sqrt(2.0 * FD)
    for d in range(9):
        for i in range(FD if d < 8 else 8):
            f = d * FD + i
            j = (i + d) % FD
            e1[i, f] = 1.0
            e2[j, f] = 1.0
            coef[f] = 1.0 / 32.0 if d == 0 else 1.0 / 16.0
            for a, b in {(i, j), (j, i)}:
                g = 1 + FD + a * FD + b
                fold[f, g] = 1.0
                spread[g, f] = 1.0
                spread_scale[g, 0] = 1.0 / (coef[f] * root * norm)
            fold_scale[f, 0] = norm / root
    b1[136] = 1.0
    coef[136] = 1.0
    fold[136, 0] = 1.0
    fold_scale[136, 0] = norm
    spread[0, 136] = 1.0
    spread_scale[0, 0] = 1.0 / norm
    for i in range(FD):
        f = 144 + i
        e1[i, f] = 1.0
        b2[f] = 1.0
        coef[f] = 0.25
        fold[f, 1 + i] = 1.0
        fold_scale[f, 0] = norm / 2.0
        spread[1 + i, f] = 1.0
        spread_scale[1 + i, 0] = 2.0 / norm
    q1 = np.zeros((128, HD * 256), np.float32)
    q2 = np.zeros((128, HD * 256), np.float32)
    k1 = np.zeros((HD * 256, 128), np.float32)
    k2 = np.zeros((HD * 256, 128), np.float32)
    for h in range(HD):
        cols = slice(256 * h, 256 * h + 256)
        q1[16 * h : 16 * h + 16, cols] = e1
        q2[16 * h : 16 * h + 16, cols] = e2
        k1[cols, 64 + 16 * h : 80 + 16 * h] = (e1 * coef).T
        k2[cols, 64 + 16 * h : 80 + 16 * h] = e2.T
    bq = np.stack([np.tile(b1, HD), np.tile(b2, HD)])
    bk = np.stack([np.tile(b1 * coef, HD), np.tile(b2, HD)], axis=1)
    pack = np.zeros((HD * 128, HD * HV), np.float32)
    pack_n = np.zeros((HD * 128, 128), np.float32)
    for h in range(HD):
        for j in range(HV):
            pack[128 * h + j, HV * h + j] = 1.0
        pack_n[128 * h + HV, h] = 1.0
    bf = lambda x: jnp.asarray(x, BF16)
    f32 = lambda x: jnp.asarray(x, F32)
    return (
        bf(q1), bf(q2), bf(k1), bf(k2), f32(bq), f32(bk), bf(fold), f32(fold_scale), bf(spread),
        f32(spread_scale), bf(pack), bf(pack.T), bf(pack_n), bf(pack_n.T[:HD]),
    )


def dot(a, b):
    return jnp.dot(a, b, preferred_element_type=F32)


def kernel(
    S, Z, C,
    lengths, owner, resume, tokens, wq, wk, wv, init, norm,
    q1, q2, k1, k2, bq, bk, fold, fold_s, spread, spread_s, pack, unpack, pack_n, unpack_n,
    out, fstate, fnorm,
    gat, wsend, wrecv, wall, stage, isend, irecv, ssend, srecv, start, lsend, lrecv, csend, crecv,
    psiq, num, eacc, run, ftab,
    ends, first, inv,
    own_sem, dsend, drecv, fsend, frecv, xsend, xrecv,
):
    T = out.shape[0]
    NC = T // C
    H = C // 2
    SR = HD * ROWS // S
    PH = S // HD
    WR = wq.shape[0]
    FW = tokens.shape[1]
    me = lax.axis_index("seq")
    mz = lax.axis_index("tp")
    up, down = lax.rem(mz + 1, Z), lax.rem(mz + Z - 1, Z)

    barrier = pltpu.get_barrier_semaphore()

    def greet(i, x):
        pl.semaphore_signal(
            barrier, inc=1, device_id={"seq": lax.rem(me + i, S)}, device_id_type=MESH
        )
        return x

    lax.fori_loop(1, S, greet, 0)
    for z in (up, down):
        pl.semaphore_signal(barrier, inc=1, device_id={"tp": z}, device_id_type=MESH)

    own = pltpu.make_async_copy(tokens, gat.at[mz], own_sem)
    own.start()
    wsend[:, :64] = wq[...]
    wsend[:, 64:128] = wk[...]
    wsend[:, 128:] = dot(wv[...], unpack[...]).astype(BF16)
    full = init[0]
    hi = full.astype(BF16)
    lo = (full - hi.astype(F32)).astype(BF16)
    folded = (dot(fold[...], hi) + dot(fold[...], lo)) * fold_s[...]
    full = norm[0]
    hi = full.astype(BF16)
    lo = (full - hi.astype(F32)).astype(BF16)
    folded_n = (dot(fold[...], hi) + dot(fold[...], lo)) * fold_s[...]
    stage[...] = dot(folded.astype(BF16), unpack[...]) + dot(folded_n.astype(BF16), unpack_n[...])
    for s in range(S):
        h, k = s // PH, s % PH
        isend[s] = stage[SR * k : SR * k + SR, 128 * h : 128 * h + 128].astype(BF16)
    pl.semaphore_wait(barrier, S + 1)

    def direct(way, c):
        rows = pl.ds(c * C, C)
        return pltpu.make_async_remote_copy(
            src_ref=tokens.at[rows],
            dst_ref=gat.at[mz, rows],
            send_sem=dsend.at[way, c],
            recv_sem=drecv.at[way, c],
            device_id={"tp": up if way == 0 else down},
            device_id_type=MESH,
        )

    def onward(way, c):
        rows = pl.ds(c * C + way * H, H)
        place = gat.at[down if way == 0 else up, rows]
        return pltpu.make_async_remote_copy(
            src_ref=place,
            dst_ref=place,
            send_sem=fsend.at[way, c],
            recv_sem=frecv.at[way, c],
            device_id={"tp": up if way == 0 else down},
            device_id_type=MESH,
        )

    def exchange(src, dst, n):
        keep = pltpu.make_async_copy(src(me), dst(me), xrecv.at[n])
        keep.start()

        def send(i, x):
            peer = lax.rem(me + i, S)
            pltpu.make_async_remote_copy(
                src_ref=src(peer),
                dst_ref=dst(me),
                send_sem=xsend.at[n],
                recv_sem=xrecv.at[n],
                device_id={"seq": peer},
                device_id_type=MESH,
            ).start()
            return x

        lax.fori_loop(1, S, send, 0)

    def arrived(dst, n):
        pltpu.make_async_copy(dst, dst, xrecv.at[n]).wait()

    def sent(buf, n):
        part = buf.at[pl.ds(0, S - 1)]
        pltpu.make_async_copy(part, part, xsend.at[n]).wait()

    for c in range(3):
        for way in (0, 1):
            direct(way, c).start()
    exchange(lambda p: isend.at[p], lambda p: irecv.at[p], 0)
    exchange(lambda p: wsend, lambda p: wrecv.at[p], 1)

    total = jnp.int32(0)
    for r in range(S):
        total = total + lengths[r]
        ends[r] = total

    def count(b, x):
        before = jnp.int32(0)
        back = jnp.int32(0)
        for r in range(S):
            before = before + (ends[r] <= b * T).astype(jnp.int32)
            back = back + jnp.where(owner[r] == b, r, 0)
        first[b] = before
        inv[b] = jnp.minimum(back, S - 1)
        return x

    lax.fori_loop(0, S, count, 0)
    first[S] = jnp.int32(S)

    arrived(irecv, 0)

    def pick(b, x):
        for j in range(SLOTS):
            r = first[b] + j
            safe = jnp.minimum(r, S - 1)
            weight = jnp.where(r < S, resume[safe], 0).astype(F32)
            ssend[b, j] = (irecv[owner[safe]].astype(F32) * weight).astype(BF16)
        return x

    lax.fori_loop(0, S, pick, 0)
    exchange(lambda p: ssend.at[p], lambda p: srecv.at[p], 2)

    def relay(c):
        for way in (0, 1):
            direct(way, c).wait_recv()
            onward(way, c).start()
        if c + 3 < NC:
            for way in (0, 1):
                direct(way, c + 3).start()

    base = me * T
    req = first[me]
    stops = []
    for j in range(ENDS):
        r = req + j
        stop = ends[jnp.minimum(r, S - 1)] - base
        stops.append(jnp.where(r < S, stop, 4 * T))

    def slot_of(pos):
        slot = jnp.zeros_like(pos)
        for stop in stops:
            slot = slot + jnp.where(pos >= stop, 1, 0)
        return slot

    for c in range(4):
        relay(c)

    run[...] = jnp.zeros_like(run)
    eacc[...] = jnp.zeros_like(eacc)
    arrived(wrecv, 1)
    for s in range(S):
        wall[WR * s : WR * s + WR, :] = wrecv[s].astype(wall.dtype)
    own.wait()

    lane64 = lax.broadcasted_iota(jnp.int32, (1, 64), 1)
    lane512 = lax.broadcasted_iota(jnp.int32, (1, HD * 128), 1)
    ones_col = lax.rem(lane512, 128) == HV

    def chunk(c, x):
        @pl.when(c == 2)
        def _():
            relay(4)

        @pl.when(c == 4)
        def _():
            relay(5)

        for way in (0, 1):
            onward(way, c).wait_recv()
        rows = pl.ds(pl.multiple_of(c * C, C), C)
        acc = jnp.zeros((C, 640), F32)
        for z in range(Z):
            acc = acc + dot(gat[z, rows, :], wall[z * FW : (z + 1) * FW, :].astype(BF16))
        qk32 = acc[:, :128]
        qk = qk32.astype(BF16)
        v = jnp.where(ones_col, 1.0, acc[:, 128:].astype(BF16).astype(F32))
        qkT = jnp.transpose(qk.astype(F32)).astype(BF16)
        pq = (dot(qk, q1[...]) * (dot(qk, q2[...]) + bq[1:2, :]) + bq[0:1, :]).astype(BF16)
        psiq[rows, :] = pq
        pk = (dot(k1[...], qkT) * (dot(k2[...], qkT) + bk[:, 1:2]) + bk[:, 0:1]).astype(BF16)
        pos_col = c * C + lax.broadcasted_iota(jnp.int32, (C, 1), 0)
        pos_row = c * C + lax.broadcasted_iota(jnp.int32, (1, C), 1)
        slot_col = slot_of(pos_col)
        slot_row = slot_of(pos_row)
        slot_top = jnp.int32(0)
        slot_next = jnp.int32(0)
        for stop in stops:
            slot_top = slot_top + (c * C >= stop).astype(jnp.int32)
            slot_next = slot_next + (c * C + C >= stop).astype(jnp.int32)
        allowed = (slot_col == slot_row) & (pos_row <= pos_col)
        from_top = (slot_col == slot_top).astype(F32)
        keep = (slot_top == slot_next).astype(F32)
        q64 = qk32[:, :64].astype(BF16).astype(F32)
        for h in range(HD):
            head = (lane64 >= 16 * h) & (lane64 < 16 * h + 16)
            a = dot(jnp.where(head, q64, 0.0).astype(BF16), qkT[64:, :]) * 0.25
            weight = jnp.where(allowed, 1.0 + a + 0.5 * a * a, 0.0).astype(BF16)
            vh = v[:, 128 * h : 128 * h + 128]
            state = run[h]
            s_hi = state.astype(BF16)
            s_lo = (state - s_hi.astype(F32)).astype(BF16)
            pqh = pq[:, 256 * h : 256 * h + 256]
            both = dot(pqh, jnp.concatenate([s_hi, s_lo], axis=1))
            num[rows, 128 * h : 128 * h + 128] = dot(weight, vh.astype(BF16)) + from_top * (
                both[:, :128] + both[:, 128:]
            )
            parts = []
            for j in range(ENDS):
                mark = (slot_col == j) & (stops[j] <= T)
                parts.append(jnp.where(mark, vh, 0.0).astype(BF16))
            parts.append(jnp.where(slot_col == slot_next, vh, 0.0).astype(BF16))
            made = dot(pk[256 * h : 256 * h + 256, :], jnp.concatenate(parts, axis=1))
            eacc[h] += made[:ROWS, : ENDS * 128]
            run[h] = keep * state + made[:, ENDS * 128 :]
        return x

    lax.fori_loop(0, NC, chunk, 0)

    for s in range(S):
        h, k = s // PH, s % PH
        rows = slice(SR * k, SR * k + SR)
        lsend[s, ENDS] = run[h, rows, :].astype(BF16)
        for j in range(ENDS):
            lsend[s, j] = eacc[h, rows, 128 * j : 128 * j + 128].astype(BF16)
    exchange(lambda p: lsend.at[p], lambda p: lrecv.at[p], 3)

    arrived(srecv, 2)
    for s in range(S):
        h, k = s // PH, s % PH
        for j in range(SLOTS):
            start[h, SR * k : SR * k + SR, 128 * j : 128 * j + 128] = srecv[s, j].astype(F32)
    start[:, ROWS:, :] = jnp.zeros((HD, 256 - ROWS, SLOTS * 128), F32)

    def begin(c, x):
        rows = pl.ds(pl.multiple_of(c * C, C), C)
        slot_col = slot_of(c * C + lax.broadcasted_iota(jnp.int32, (C, 1), 0))
        for h in range(HD):
            got = dot(psiq[rows, 256 * h : 256 * h + 256], start[h].astype(BF16))
            add = jnp.zeros((C, 128), F32)
            for j in range(SLOTS):
                add = jnp.where(slot_col == j, got[:, 128 * j : 128 * j + 128], add)
            num[rows, 128 * h : 128 * h + 128] += add
        return x

    lax.fori_loop(0, NC, begin, 0)

    arrived(lrecv, 3)

    def carry(b, c):
        csend[b, 0] = c.astype(BF16)
        go_on = (first[b] == first[b + 1]).astype(F32)
        ftab[b] = c
        return c * go_on + lrecv[b, ENDS].astype(F32)

    lax.fori_loop(0, S, carry, jnp.zeros((SR, 128), F32))

    def finish(o, x):
        r = inv[o]
        b = jnp.clip(lax.div(ends[r] - 1, T), 0, S - 1)
        j = jnp.clip(r - first[b], 0, ENDS - 1)
        lead = (j == 0).astype(F32)
        csend[o, 1] = (lrecv[b, j].astype(F32) + lead * ftab[b]).astype(BF16)
        return x

    lax.fori_loop(0, S, finish, 0)
    exchange(lambda p: csend.at[p], lambda p: crecv.at[p], 4)
    arrived(crecv, 4)
    for s in range(S):
        h, k = s // PH, s % PH
        rows = slice(SR * k, SR * k + SR)
        run[h, rows, :] = crecv[s, 0].astype(F32)
        stage[rows, 128 * h : 128 * h + 128] = crecv[s, 1].astype(F32)
    run[:, ROWS:, :] = jnp.zeros((HD, 256 - ROWS, 128), F32)

    def close(c, x):
        rows = pl.ds(pl.multiple_of(c * C, C), C)
        slot_col = slot_of(c * C + lax.broadcasted_iota(jnp.int32, (C, 1), 0))
        parts = []
        for h in range(HD):
            got = dot(psiq[rows, 256 * h : 256 * h + 256], run[h].astype(BF16))
            both = num[rows, 128 * h : 128 * h + 128] + jnp.where(slot_col == 0, got, 0.0)
            parts.append((both / both[:, HV : HV + 1]).astype(BF16))
        out[rows, :] = dot(jnp.concatenate(parts, axis=1), pack[...]).astype(BF16)
        return x

    lax.fori_loop(0, NC, close, 0)

    got = stage[...].astype(BF16)
    flag = resume[inv[me]].astype(F32)
    fstate[0] = flag * init[0] + spread_s[...] * dot(spread[...], dot(got, pack[...]).astype(BF16))
    moved = spread_s[...] * dot(spread[...], dot(got, pack_n[...]).astype(BF16))
    fnorm[0] = flag * norm[0] + moved[:, :HD]

    for c in range(NC):
        for way in (0, 1):
            direct(way, c).wait_send()
            onward(way, c).wait_send()
    for n, buf in ((0, isend), (1, wrecv), (2, ssend), (3, lsend), (4, csend)):
        sent(buf, n)


def local(tokens, wq, wk, wv, lengths, owner, resume, init, norm):
    S, Z = lax.axis_size("seq"), lax.axis_size("tp")
    T, FW = tokens.shape
    C = T // 6
    SR = HD * ROWS // S
    consts = tables(float(T * S // 2))
    smem = pl.BlockSpec(memory_space=pltpu.SMEM)
    vmem = pl.BlockSpec(memory_space=pltpu.VMEM)
    hbm = pl.BlockSpec(memory_space=pl.ANY)
    return pl.pallas_call(
        functools.partial(kernel, S, Z, C),
        out_shape=(
            jax.ShapeDtypeStruct((T, HD * HV), BF16),
            jax.ShapeDtypeStruct(init.shape, F32),
            jax.ShapeDtypeStruct(norm.shape, F32),
        ),
        in_specs=[smem] * 3 + [hbm] + [vmem] * (5 + len(consts)),
        out_specs=(vmem, vmem, vmem),
        scratch_shapes=[
            pltpu.VMEM((Z, T, FW), BF16),
            pltpu.VMEM((wq.shape[0], 640), BF16),
            pltpu.VMEM((S, wq.shape[0], 640), BF16),
            pltpu.VMEM((S * wq.shape[0], 640), F32),
            pltpu.VMEM((ROWS, HD * 128), F32),
            pltpu.VMEM((S, SR, 128), BF16),
            pltpu.VMEM((S, SR, 128), BF16),
            pltpu.VMEM((S, SLOTS, SR, 128), BF16),
            pltpu.VMEM((S, SLOTS, SR, 128), BF16),
            pltpu.VMEM((HD, 256, SLOTS * 128), F32),
            pltpu.VMEM((S, SLOTS, SR, 128), BF16),
            pltpu.VMEM((S, SLOTS, SR, 128), BF16),
            pltpu.VMEM((S, 2, SR, 128), BF16),
            pltpu.VMEM((S, 2, SR, 128), BF16),
            pltpu.VMEM((T, HD * 256), BF16),
            pltpu.VMEM((T, HD * 128), F32),
            pltpu.VMEM((HD, ROWS, ENDS * 128), F32),
            pltpu.VMEM((HD, 256, 128), F32),
            pltpu.VMEM((S, SR, 128), F32),
            pltpu.SMEM((S,), jnp.int32),
            pltpu.SMEM((S + 1,), jnp.int32),
            pltpu.SMEM((S,), jnp.int32),
            pltpu.SemaphoreType.DMA,
            pltpu.SemaphoreType.DMA((2, 6)),
            pltpu.SemaphoreType.DMA((2, 6)),
            pltpu.SemaphoreType.DMA((2, 6)),
            pltpu.SemaphoreType.DMA((2, 6)),
            pltpu.SemaphoreType.DMA((5,)),
            pltpu.SemaphoreType.DMA((5,)),
        ],
        compiler_params=pltpu.CompilerParams(
            collective_id=0, has_side_effects=True, vmem_limit_bytes=60 * 2**20
        ),
    )(lengths, owner, resume, tokens, wq, wk, wv, init, norm, *consts)


def solution(mesh):
    in_specs = (
        P("seq", "tp"),
        P("seq", "tp"),
        P("seq", "tp"),
        P("seq", "tp"),
        P(),
        P(),
        P(),
        P("seq", None, "tp"),
        P("seq", None, "tp"),
    )
    out_specs = (P("seq", "tp"), P("seq", None, "tp"), P("seq", None, "tp"))
    return jax.shard_map(local, mesh=mesh, in_specs=in_specs, out_specs=out_specs, check_vma=False)
```

```python
import functools
import math

import jax
import jax.numpy as jnp
import numpy as np
from jax import lax
from jax.experimental import pallas as pl
from jax.experimental.pallas import tpu as pltpu
from jax.sharding import PartitionSpec as P

FD = 16
HD = 4
HV = 112
FEAT = 273
ENDS = 4
SLOTS = 5
ROWS = 192
MESH = pl.DeviceIdType.MESH
F32 = jnp.float32
BF16 = jnp.bfloat16


def tables(norm):
    e1 = np.zeros((FD, 256), np.float32)
    e2 = np.zeros((FD, 256), np.float32)
    b1 = np.zeros((256,), np.float32)
    b2 = np.zeros((256,), np.float32)
    coef = np.zeros((256,), np.float32)
    fold = np.zeros((ROWS, FEAT), np.float32)
    fold_scale = np.zeros((ROWS, 1), np.float32)
    spread = np.zeros((FEAT, ROWS), np.float32)
    spread_scale = np.zeros((FEAT, 1), np.float32)
    root = math.sqrt(2.0 * FD)
    for d in range(9):
        for i in range(FD if d < 8 else 8):
            f = d * FD + i
            j = (i + d) % FD
            e1[i, f] = 1.0
            e2[j, f] = 1.0
            coef[f] = 1.0 / 32.0 if d == 0 else 1.0 / 16.0
            for a, b in {(i, j), (j, i)}:
                g = 1 + FD + a * FD + b
                fold[f, g] = 1.0
                spread[g, f] = 1.0
                spread_scale[g, 0] = 1.0 / (coef[f] * root * norm)
            fold_scale[f, 0] = norm / root
    b1[136] = 1.0
    coef[136] = 1.0
    fold[136, 0] = 1.0
    fold_scale[136, 0] = norm
    spread[0, 136] = 1.0
    spread_scale[0, 0] = 1.0 / norm
    for i in range(FD):
        f = 144 + i
        e1[i, f] = 1.0
        b2[f] = 1.0
        coef[f] = 0.25
        fold[f, 1 + i] = 1.0
        fold_scale[f, 0] = norm / 2.0
        spread[1 + i, f] = 1.0
        spread_scale[1 + i, 0] = 2.0 / norm
    q1 = np.zeros((128, HD * 256), np.float32)
    q2 = np.zeros((128, HD * 256), np.float32)
    k1 = np.zeros((HD * 256, 128), np.float32)
    k2 = np.zeros((HD * 256, 128), np.float32)
    for h in range(HD):
        cols = slice(256 * h, 256 * h + 256)
        q1[16 * h : 16 * h + 16, cols] = e1
        q2[16 * h : 16 * h + 16, cols] = e2
        k1[cols, 64 + 16 * h : 80 + 16 * h] = (e1 * coef).T
        k2[cols, 64 + 16 * h : 80 + 16 * h] = e2.T
    bq = np.stack([np.tile(b1, HD), np.tile(b2, HD)])
    bk = np.stack([np.tile(b1 * coef, HD), np.tile(b2, HD)], axis=1)
    pack = np.zeros((HD * 128, HD * HV), np.float32)
    pack_n = np.zeros((HD * 128, 128), np.float32)
    for h in range(HD):
        for j in range(HV):
            pack[128 * h + j, HV * h + j] = 1.0
        pack_n[128 * h + HV, h] = 1.0
    bf = lambda x: jnp.asarray(x, BF16)
    f32 = lambda x: jnp.asarray(x, F32)
    return (
        bf(q1), bf(q2), bf(k1), bf(k2), f32(bq), f32(bk), bf(fold), f32(fold_scale), bf(spread),
        f32(spread_scale), f32(spread_scale.T), bf(pack), bf(pack.T), bf(pack_n.T[:HD]),
    )


def dot(a, b):
    return jnp.dot(a, b, preferred_element_type=F32)


def dot_nt(a, b):
    return lax.dot_general(a, b, (((1,), (1,)), ((), ())), preferred_element_type=F32)


def kernel(
    S, Z, C,
    lengths, owner, resume, tokens, wq, wk, wv, init, norm,
    q1, q2, k1, k2, bq, bk, fold, fold_s, spread, spread_s, spread_t, pack, unpack, unpack_n,
    out, fstate, fnorm,
    gat, wsend, wrecv, wall, wallt, stage, isend, irecv, ssend, srecv, start, lsend, lrecv, csend, crecv,
    psiq, num, eacc, run, ftab,
    ends, first, inv,
    own_sem, dsend, drecv, fsend, frecv, xsend, xrecv,
):
    T = out.shape[1]
    NC = T // C
    H = C // 2
    SR = HD * ROWS // S
    PH = S // HD
    WR = wq.shape[0]
    FW = tokens.shape[0]
    me = lax.axis_index("seq")
    mz = lax.axis_index("tp")
    up, down = lax.rem(mz + 1, Z), lax.rem(mz + Z - 1, Z)

    barrier = pltpu.get_barrier_semaphore()

    def greet(i, x):
        pl.semaphore_signal(
            barrier, inc=1, device_id={"seq": lax.rem(me + i, S)}, device_id_type=MESH
        )
        return x

    lax.fori_loop(1, S, greet, 0)
    for z in (up, down):
        pl.semaphore_signal(barrier, inc=1, device_id={"tp": z}, device_id_type=MESH)

    own = pltpu.make_async_copy(tokens, gat.at[mz], own_sem)
    own.start()
    wsend[:, :64] = wq[...]
    wsend[:, 64:128] = wk[...]
    wsend[:, 128:] = dot(wv[...], unpack[...]).astype(BF16)
    full = init[0]
    hi = full.astype(BF16)
    lo = (full - hi.astype(F32)).astype(BF16)
    folded = (dot(fold[...], hi) + dot(fold[...], lo)) * fold_s[...]
    full = norm[0]
    hi = full.astype(BF16)
    lo = (full - hi.astype(F32)).astype(BF16)
    folded_n = (dot_nt(fold[...], hi) + dot_nt(fold[...], lo)) * fold_s[...]
    stage[...] = dot(folded.astype(BF16), unpack[...]) + dot(folded_n.astype(BF16), unpack_n[...])
    for s in range(S):
        h, k = s // PH, s % PH
        isend[s] = stage[SR * k : SR * k + SR, 128 * h : 128 * h + 128].astype(BF16)
    pl.semaphore_wait(barrier, S + 1)

    def direct(way, c):
        rows = pl.ds(c * C, C)
        return pltpu.make_async_remote_copy(
            src_ref=tokens.at[:, rows],
            dst_ref=gat.at[mz, :, rows],
            send_sem=dsend.at[way, c],
            recv_sem=drecv.at[way, c],
            device_id={"tp": up if way == 0 else down},
            device_id_type=MESH,
        )

    def onward(way, c):
        rows = pl.ds(c * C + way * H, H)
        place = gat.at[down if way == 0 else up, :, rows]
        return pltpu.make_async_remote_copy(
            src_ref=place,
            dst_ref=place,
            send_sem=fsend.at[way, c],
            recv_sem=frecv.at[way, c],
            device_id={"tp": up if way == 0 else down},
            device_id_type=MESH,
        )

    def exchange(src, dst, n):
        keep = pltpu.make_async_copy(src(me), dst(me), xrecv.at[n])
        keep.start()

        def send(i, x):
            peer = lax.rem(me + i, S)
            pltpu.make_async_remote_copy(
                src_ref=src(peer),
                dst_ref=dst(me),
                send_sem=xsend.at[n],
                recv_sem=xrecv.at[n],
                device_id={"seq": peer},
                device_id_type=MESH,
            ).start()
            return x

        lax.fori_loop(1, S, send, 0)

    def arrived(dst, n):
        pltpu.make_async_copy(dst, dst, xrecv.at[n]).wait()

    def sent(buf, n):
        part = buf.at[pl.ds(0, S - 1)]
        pltpu.make_async_copy(part, part, xsend.at[n]).wait()

    for c in range(3):
        for way in (0, 1):
            direct(way, c).start()
    exchange(lambda p: isend.at[p], lambda p: irecv.at[p], 0)
    exchange(lambda p: wsend, lambda p: wrecv.at[p], 1)

    total = jnp.int32(0)
    for r in range(S):
        total = total + lengths[r]
        ends[r] = total

    def count(b, x):
        before = jnp.int32(0)
        back = jnp.int32(0)
        for r in range(S):
            before = before + (ends[r] <= b * T).astype(jnp.int32)
            back = back + jnp.where(owner[r] == b, r, 0)
        first[b] = before
        inv[b] = jnp.minimum(back, S - 1)
        return x

    lax.fori_loop(0, S, count, 0)
    first[S] = jnp.int32(S)

    arrived(irecv, 0)

    def pick(b, x):
        for j in range(SLOTS):
            r = first[b] + j
            safe = jnp.minimum(r, S - 1)
            weight = jnp.where(r < S, resume[safe], 0).astype(F32)
            ssend[b, j] = (irecv[owner[safe]].astype(F32) * weight).astype(BF16)
        return x

    lax.fori_loop(0, S, pick, 0)
    exchange(lambda p: ssend.at[p], lambda p: srecv.at[p], 2)

    def relay(c):
        for way in (0, 1):
            direct(way, c).wait_recv()
            onward(way, c).start()
        if c + 3 < NC:
            for way in (0, 1):
                direct(way, c + 3).start()

    base = me * T
    req = first[me]
    stops = []
    for j in range(ENDS):
        r = req + j
        stop = ends[jnp.minimum(r, S - 1)] - base
        stops.append(jnp.where(r < S, stop, 4 * T))

    def slot_of(pos):
        slot = jnp.zeros_like(pos)
        for stop in stops:
            slot = slot + jnp.where(pos >= stop, 1, 0)
        return slot

    for c in range(4):
        relay(c)

    run[...] = jnp.zeros_like(run)
    eacc[...] = jnp.zeros_like(eacc)
    arrived(wrecv, 1)
    for s in range(S):
        wall[WR * s : WR * s + WR, :] = wrecv[s].astype(wall.dtype)
    for z in range(Z):
        wallt[z] = jnp.transpose(wall[z * FW : (z + 1) * FW, :]).astype(BF16)
    own.wait()

    lane64 = lax.broadcasted_iota(jnp.int32, (1, 64), 1)
    ones_row = lax.broadcasted_iota(jnp.int32, (128, 1), 0) == HV

    def chunk(c, x):
        @pl.when(c == 2)
        def _():
            relay(4)

        @pl.when(c == 4)
        def _():
            relay(5)

        for way in (0, 1):
            onward(way, c).wait_recv()
        rows = pl.ds(pl.multiple_of(c * C, C), C)
        acc = jnp.zeros((640, C), F32)
        for z in range(Z):
            acc = acc + dot(wallt[z], gat[z, :, rows])
        qkT = acc[:128].astype(BF16)
        qk32 = jnp.transpose(acc[:128])
        qk = qk32.astype(BF16)
        pq = (dot(qk, q1[...]) * (dot(qk, q2[...]) + bq[1:2, :]) + bq[0:1, :]).astype(BF16)
        psiq[rows, :] = pq
        pk = (dot(k1[...], qkT) * (dot(k2[...], qkT) + bk[:, 1:2]) + bk[:, 0:1]).astype(BF16)
        pos_col = c * C + lax.broadcasted_iota(jnp.int32, (C, 1), 0)
        pos_row = c * C + lax.broadcasted_iota(jnp.int32, (1, C), 1)
        slot_col = slot_of(pos_col)
        slot_row = slot_of(pos_row)
        slot_top = jnp.int32(0)
        slot_next = jnp.int32(0)
        for stop in stops:
            slot_top = slot_top + (c * C >= stop).astype(jnp.int32)
            slot_next = slot_next + (c * C + C >= stop).astype(jnp.int32)
        allowed = (slot_col == slot_row) & (pos_row <= pos_col)
        from_top = (slot_col == slot_top).astype(F32)
        keep = (slot_top == slot_next).astype(F32)
        q64 = qk32[:, :64].astype(BF16).astype(F32)
        for h in range(HD):
            head = (lane64 >= 16 * h) & (lane64 < 16 * h + 16)
            a = dot(jnp.where(head, q64, 0.0).astype(BF16), qkT[64:, :]) * 0.25
            weight = jnp.where(allowed, 1.0 + a + 0.5 * a * a, 0.0).astype(BF16)
            vh = jnp.where(ones_row, 1.0, acc[128 * h + 128 : 128 * h + 256])
            state = run[h]
            s_hi = state.astype(BF16)
            s_lo = (state - s_hi.astype(F32)).astype(BF16)
            pqh = pq[:, 256 * h : 256 * h + 256]
            both = dot(pqh, jnp.concatenate([s_hi, s_lo], axis=1))
            num[rows, 128 * h : 128 * h + 128] = dot_nt(weight, vh.astype(BF16)) + from_top * (
                both[:, :128] + both[:, 128:]
            )
            parts = []
            for j in range(ENDS):
                mark = (slot_row == j) & (stops[j] <= T)
                parts.append(jnp.where(mark, vh, 0.0).astype(BF16))
            parts.append(jnp.where(slot_row == slot_next, vh, 0.0).astype(BF16))
            made = dot_nt(pk[256 * h : 256 * h + 256, :], jnp.concatenate(parts, axis=0))
            eacc[h] += made[:ROWS, : ENDS * 128]
            run[h] = keep * state + made[:, ENDS * 128 :]
        return x

    lax.fori_loop(0, NC, chunk, 0)

    for s in range(S):
        h, k = s // PH, s % PH
        rows = slice(SR * k, SR * k + SR)
        lsend[s, ENDS] = run[h, rows, :].astype(BF16)
        for j in range(ENDS):
            lsend[s, j] = eacc[h, rows, 128 * j : 128 * j + 128].astype(BF16)
    exchange(lambda p: lsend.at[p], lambda p: lrecv.at[p], 3)

    arrived(srecv, 2)
    for s in range(S):
        h, k = s // PH, s % PH
        for j in range(SLOTS):
            start[h, SR * k : SR * k + SR, 128 * j : 128 * j + 128] = srecv[s, j].astype(F32)
    start[:, ROWS:, :] = jnp.zeros((HD, 256 - ROWS, SLOTS * 128), F32)

    def begin(c, x):
        rows = pl.ds(pl.multiple_of(c * C, C), C)
        slot_col = slot_of(c * C + lax.broadcasted_iota(jnp.int32, (C, 1), 0))
        for h in range(HD):
            got = dot(psiq[rows, 256 * h : 256 * h + 256], start[h].astype(BF16))
            add = jnp.zeros((C, 128), F32)
            for j in range(SLOTS):
                add = jnp.where(slot_col == j, got[:, 128 * j : 128 * j + 128], add)
            num[rows, 128 * h : 128 * h + 128] += add
        return x

    lax.fori_loop(0, NC, begin, 0)

    arrived(lrecv, 3)

    def carry(b, c):
        csend[b, 0] = c.astype(BF16)
        go_on = (first[b] == first[b + 1]).astype(F32)
        ftab[b] = c
        return c * go_on + lrecv[b, ENDS].astype(F32)

    lax.fori_loop(0, S, carry, jnp.zeros((SR, 128), F32))

    def finish(o, x):
        r = inv[o]
        b = jnp.clip(lax.div(ends[r] - 1, T), 0, S - 1)
        j = jnp.clip(r - first[b], 0, ENDS - 1)
        lead = (j == 0).astype(F32)
        csend[o, 1] = (lrecv[b, j].astype(F32) + lead * ftab[b]).astype(BF16)
        return x

    lax.fori_loop(0, S, finish, 0)
    exchange(lambda p: csend.at[p], lambda p: crecv.at[p], 4)
    arrived(crecv, 4)
    for s in range(S):
        h, k = s // PH, s % PH
        rows = slice(SR * k, SR * k + SR)
        run[h, rows, :] = crecv[s, 0].astype(F32)
        stage[rows, 128 * h : 128 * h + 128] = crecv[s, 1].astype(F32)
    run[:, ROWS:, :] = jnp.zeros((HD, 256 - ROWS, 128), F32)

    def close(c, x):
        rows = pl.ds(pl.multiple_of(c * C, C), C)
        slot_col = slot_of(c * C + lax.broadcasted_iota(jnp.int32, (C, 1), 0))
        parts = []
        for h in range(HD):
            got = dot(psiq[rows, 256 * h : 256 * h + 256], run[h].astype(BF16))
            both = num[rows, 128 * h : 128 * h + 128] + jnp.where(slot_col == 0, got, 0.0)
            parts.append((both / both[:, HV : HV + 1]).astype(BF16))
        out[:, rows] = dot_nt(unpack[...], jnp.concatenate(parts, axis=1)).astype(BF16)
        return x

    lax.fori_loop(0, NC, close, 0)

    got = stage[...].astype(BF16)
    flag = resume[inv[me]].astype(F32)
    fstate[0] = flag * init[0] + spread_s[...] * dot(spread[...], dot(got, pack[...]).astype(BF16))
    moved = spread_t[...] * dot_nt(dot_nt(unpack_n[...], got).astype(BF16), spread[...])
    fnorm[0] = flag * norm[0] + moved

    for c in range(NC):
        for way in (0, 1):
            direct(way, c).wait_send()
            onward(way, c).wait_send()
    for n, buf in ((0, isend), (1, wrecv), (2, ssend), (3, lsend), (4, csend)):
        sent(buf, n)


def local(tokens, wq, wk, wv, lengths, owner, resume, init, norm):
    S, Z = lax.axis_size("seq"), lax.axis_size("tp")
    tokens, norm = tokens.T, jnp.transpose(norm, (0, 2, 1))
    FW, T = tokens.shape
    C = T // 6
    SR = HD * ROWS // S
    consts = tables(float(T * S // 2))
    smem = pl.BlockSpec(memory_space=pltpu.SMEM)
    vmem = pl.BlockSpec(memory_space=pltpu.VMEM)
    hbm = pl.BlockSpec(memory_space=pl.ANY)
    out, state, moved = pl.pallas_call(
        functools.partial(kernel, S, Z, C),
        out_shape=(
            jax.ShapeDtypeStruct((HD * HV, T), BF16),
            jax.ShapeDtypeStruct(init.shape, F32),
            jax.ShapeDtypeStruct(norm.shape, F32),
        ),
        in_specs=[smem] * 3 + [hbm] + [vmem] * (5 + len(consts)),
        out_specs=(vmem, vmem, vmem),
        scratch_shapes=[
            pltpu.VMEM((Z, FW, T), BF16),
            pltpu.VMEM((wq.shape[0], 640), BF16),
            pltpu.VMEM((S, wq.shape[0], 640), BF16),
            pltpu.VMEM((S * wq.shape[0], 640), F32),
            pltpu.VMEM((Z, 640, FW), BF16),
            pltpu.VMEM((ROWS, HD * 128), F32),
            pltpu.VMEM((S, SR, 128), BF16),
            pltpu.VMEM((S, SR, 128), BF16),
            pltpu.VMEM((S, SLOTS, SR, 128), BF16),
            pltpu.VMEM((S, SLOTS, SR, 128), BF16),
            pltpu.VMEM((HD, 256, SLOTS * 128), F32),
            pltpu.VMEM((S, SLOTS, SR, 128), BF16),
            pltpu.VMEM((S, SLOTS, SR, 128), BF16),
            pltpu.VMEM((S, 2, SR, 128), BF16),
            pltpu.VMEM((S, 2, SR, 128), BF16),
            pltpu.VMEM((T, HD * 256), BF16),
            pltpu.VMEM((T, HD * 128), F32),
            pltpu.VMEM((HD, ROWS, ENDS * 128), F32),
            pltpu.VMEM((HD, 256, 128), F32),
            pltpu.VMEM((S, SR, 128), F32),
            pltpu.SMEM((S,), jnp.int32),
            pltpu.SMEM((S + 1,), jnp.int32),
            pltpu.SMEM((S,), jnp.int32),
            pltpu.SemaphoreType.DMA,
            pltpu.SemaphoreType.DMA((2, 6)),
            pltpu.SemaphoreType.DMA((2, 6)),
            pltpu.SemaphoreType.DMA((2, 6)),
            pltpu.SemaphoreType.DMA((2, 6)),
            pltpu.SemaphoreType.DMA((5,)),
            pltpu.SemaphoreType.DMA((5,)),
        ],
        compiler_params=pltpu.CompilerParams(
            collective_id=0, has_side_effects=True, vmem_limit_bytes=60 * 2**20
        ),
    )(lengths, owner, resume, tokens, wq, wk, wv, init, norm, *consts)
    return out.T, state, jnp.transpose(moved, (0, 2, 1))


def solution(mesh):
    in_specs = (
        P("seq", "tp"),
        P("seq", "tp"),
        P("seq", "tp"),
        P("seq", "tp"),
        P(),
        P(),
        P(),
        P("seq", None, "tp"),
        P("seq", None, "tp"),
    )
    out_specs = (P("seq", "tp"), P("seq", None, "tp"), P("seq", None, "tp"))
    return jax.shard_map(local, mesh=mesh, in_specs=in_specs, out_specs=out_specs, check_vma=False)
```

```python
import functools
import math

import jax
import jax.numpy as jnp
import numpy as np
from jax import lax
from jax.experimental import pallas as pl
from jax.experimental.pallas import tpu as pltpu
from jax.sharding import PartitionSpec as P

FD = 16
HD = 4
HV = 112
FEAT = 273
ENDS = 4
SLOTS = 5
ROWS = 192
MESH = pl.DeviceIdType.MESH
F32 = jnp.float32
BF16 = jnp.bfloat16


def tables(norm):
    e1 = np.zeros((FD, 256), np.float32)
    e2 = np.zeros((FD, 256), np.float32)
    b1 = np.zeros((256,), np.float32)
    b2 = np.zeros((256,), np.float32)
    coef = np.zeros((256,), np.float32)
    fold = np.zeros((ROWS, FEAT), np.float32)
    fold_scale = np.zeros((ROWS, 1), np.float32)
    spread = np.zeros((FEAT, ROWS), np.float32)
    spread_scale = np.zeros((FEAT, 1), np.float32)
    root = math.sqrt(2.0 * FD)
    for d in range(9):
        for i in range(FD if d < 8 else 8):
            f = d * FD + i
            j = (i + d) % FD
            e1[i, f] = 1.0
            e2[j, f] = 1.0
            coef[f] = 1.0 / 32.0 if d == 0 else 1.0 / 16.0
            for a, b in {(i, j), (j, i)}:
                g = 1 + FD + a * FD + b
                fold[f, g] = 1.0
                spread[g, f] = 1.0
                spread_scale[g, 0] = 1.0 / (coef[f] * root * norm)
            fold_scale[f, 0] = norm / root
    b1[136] = 1.0
    coef[136] = 1.0
    fold[136, 0] = 1.0
    fold_scale[136, 0] = norm
    spread[0, 136] = 1.0
    spread_scale[0, 0] = 1.0 / norm
    for i in range(FD):
        f = 144 + i
        e1[i, f] = 1.0
        b2[f] = 1.0
        coef[f] = 0.25
        fold[f, 1 + i] = 1.0
        fold_scale[f, 0] = norm / 2.0
        spread[1 + i, f] = 1.0
        spread_scale[1 + i, 0] = 2.0 / norm
    q1 = np.zeros((128, HD * 256), np.float32)
    q2 = np.zeros((128, HD * 256), np.float32)
    k1 = np.zeros((HD * 256, 128), np.float32)
    k2 = np.zeros((HD * 256, 128), np.float32)
    for h in range(HD):
        cols = slice(256 * h, 256 * h + 256)
        q1[16 * h : 16 * h + 16, cols] = e1
        q2[16 * h : 16 * h + 16, cols] = e2
        k1[cols, 64 + 16 * h : 80 + 16 * h] = (e1 * coef).T
        k2[cols, 64 + 16 * h : 80 + 16 * h] = e2.T
    bq = np.stack([np.tile(b1, HD), np.tile(b2, HD)])
    bk = np.stack([np.tile(b1 * coef, HD), np.tile(b2, HD)], axis=1)
    pack = np.zeros((HD * 128, HD * HV), np.float32)
    pack_n = np.zeros((HD * 128, 128), np.float32)
    for h in range(HD):
        for j in range(HV):
            pack[128 * h + j, HV * h + j] = 1.0
        pack_n[128 * h + HV, h] = 1.0
    bf = lambda x: jnp.asarray(x, BF16)
    f32 = lambda x: jnp.asarray(x, F32)
    return (
        bf(q1), bf(q2), bf(k1), bf(k2), f32(bq), f32(bk), bf(fold), f32(fold_scale), bf(spread),
        f32(spread_scale), f32(spread_scale.T), bf(pack), bf(pack.T), bf(pack_n.T[:HD]),
    )


def dot(a, b):
    return jnp.dot(a, b, preferred_element_type=F32)


def dot_nt(a, b):
    return lax.dot_general(a, b, (((1,), (1,)), ((), ())), preferred_element_type=F32)


def kernel(
    S, Z, C,
    lengths, owner, resume, tokens, wq, wk, wv, init, norm,
    q1, q2, k1, k2, bq, bk, fold, fold_s, spread, spread_s, spread_t, pack, unpack, unpack_n,
    out, fstate, fnorm,
    gat, wsend, wrecv, wall, wallb, stage, isend, irecv, ssend, srecv, start, lsend, lrecv, csend, crecv,
    psiq, num, eacc, run, ftab,
    ends, first, inv,
    own_sem, dsend, drecv, fsend, frecv, xsend, xrecv,
):
    T = out.shape[0]
    NC = T // C
    H = C // 2
    SR = HD * ROWS // S
    PH = S // HD
    WR = wq.shape[0]
    FW = tokens.shape[1]
    me = lax.axis_index("seq")
    mz = lax.axis_index("tp")
    up, down = lax.rem(mz + 1, Z), lax.rem(mz + Z - 1, Z)

    barrier = pltpu.get_barrier_semaphore()

    def greet(i, x):
        pl.semaphore_signal(
            barrier, inc=1, device_id={"seq": lax.rem(me + i, S)}, device_id_type=MESH
        )
        return x

    lax.fori_loop(1, S, greet, 0)
    for z in (up, down):
        pl.semaphore_signal(barrier, inc=1, device_id={"tp": z}, device_id_type=MESH)

    own = pltpu.make_async_copy(tokens, gat.at[mz], own_sem)
    own.start()
    wsend[:, :64] = wq[...]
    wsend[:, 64:128] = wk[...]
    wsend[:, 128:] = dot(wv[...], unpack[...]).astype(BF16)
    full = init[0]
    hi = full.astype(BF16)
    lo = (full - hi.astype(F32)).astype(BF16)
    folded = (dot(fold[...], hi) + dot(fold[...], lo)) * fold_s[...]
    full = norm[0]
    hi = full.astype(BF16)
    lo = (full - hi.astype(F32)).astype(BF16)
    folded_n = (dot_nt(fold[...], hi) + dot_nt(fold[...], lo)) * fold_s[...]
    stage[...] = dot(folded.astype(BF16), unpack[...]) + dot(folded_n.astype(BF16), unpack_n[...])
    for s in range(S):
        h, k = s // PH, s % PH
        isend[s] = stage[SR * k : SR * k + SR, 128 * h : 128 * h + 128].astype(BF16)
    pl.semaphore_wait(barrier, S + 1)

    def direct(way, c):
        rows = pl.ds(c * C, C)
        return pltpu.make_async_remote_copy(
            src_ref=tokens.at[rows],
            dst_ref=gat.at[mz, rows],
            send_sem=dsend.at[way, c],
            recv_sem=drecv.at[way, c],
            device_id={"tp": up if way == 0 else down},
            device_id_type=MESH,
        )

    def onward(way, c):
        rows = pl.ds(c * C + way * H, H)
        place = gat.at[down if way == 0 else up, rows]
        return pltpu.make_async_remote_copy(
            src_ref=place,
            dst_ref=place,
            send_sem=fsend.at[way, c],
            recv_sem=frecv.at[way, c],
            device_id={"tp": up if way == 0 else down},
            device_id_type=MESH,
        )

    def exchange(src, dst, n):
        keep = pltpu.make_async_copy(src(me), dst(me), xrecv.at[n])
        keep.start()

        def send(i, x):
            peer = lax.rem(me + i, S)
            pltpu.make_async_remote_copy(
                src_ref=src(peer),
                dst_ref=dst(me),
                send_sem=xsend.at[n],
                recv_sem=xrecv.at[n],
                device_id={"seq": peer},
                device_id_type=MESH,
            ).start()
            return x

        lax.fori_loop(1, S, send, 0)

    def arrived(dst, n):
        pltpu.make_async_copy(dst, dst, xrecv.at[n]).wait()

    def sent(buf, n):
        part = buf.at[pl.ds(0, S - 1)]
        pltpu.make_async_copy(part, part, xsend.at[n]).wait()

    side = lax.rem(me, 2)
    twin = me + 1 - 2 * side

    def spread_weights():
        pltpu.make_async_copy(wsend, wrecv.at[me], xrecv.at[1]).start()

        def send(i, x):
            pltpu.make_async_remote_copy(
                src_ref=wsend,
                dst_ref=wrecv.at[me],
                send_sem=xsend.at[1],
                recv_sem=xrecv.at[1],
                device_id={"seq": lax.rem(me + 2 * i, S)},
                device_id_type=MESH,
            ).start()
            return x

        lax.fori_loop(1, S // 2, send, 0)

    def half_arrived(n):
        part = wrecv.at[pl.ds(0, S // 2)]
        pltpu.make_async_copy(part, part, xrecv.at[n]).wait()

    def share_weights():
        half_arrived(1)

        def send(i, x):
            place = wrecv.at[2 * i + side]
            pltpu.make_async_remote_copy(
                src_ref=place,
                dst_ref=place,
                send_sem=xsend.at[5],
                recv_sem=xrecv.at[5],
                device_id={"seq": twin},
                device_id_type=MESH,
            ).start()
            return x

        lax.fori_loop(0, S // 2, send, 0)

    for c in range(3):
        for way in (0, 1):
            direct(way, c).start()
    spread_weights()
    exchange(lambda p: isend.at[p], lambda p: irecv.at[p], 0)

    total = jnp.int32(0)
    for r in range(S):
        total = total + lengths[r]
        ends[r] = total

    def count(b, x):
        before = jnp.int32(0)
        back = jnp.int32(0)
        for r in range(S):
            before = before + (ends[r] <= b * T).astype(jnp.int32)
            back = back + jnp.where(owner[r] == b, r, 0)
        first[b] = before
        inv[b] = jnp.minimum(back, S - 1)
        return x

    lax.fori_loop(0, S, count, 0)
    first[S] = jnp.int32(S)

    arrived(irecv, 0)

    def pick(b, x):
        for j in range(SLOTS):
            r = first[b] + j
            safe = jnp.minimum(r, S - 1)
            weight = jnp.where(r < S, resume[safe], 0).astype(F32)
            ssend[b, j] = (irecv[owner[safe]].astype(F32) * weight).astype(BF16)
        return x

    lax.fori_loop(0, S, pick, 0)

    def relay(c):
        for way in (0, 1):
            direct(way, c).wait_recv()
            onward(way, c).start()
        if c + 3 < NC:
            for way in (0, 1):
                direct(way, c + 3).start()

    base = me * T
    req = first[me]
    stops = []
    for j in range(ENDS):
        r = req + j
        stop = ends[jnp.minimum(r, S - 1)] - base
        stops.append(jnp.where(r < S, stop, 4 * T))

    def slot_of(pos):
        slot = jnp.zeros_like(pos)
        for stop in stops:
            slot = slot + jnp.where(pos >= stop, 1, 0)
        return slot

    for c in range(2):
        relay(c)
    share_weights()
    exchange(lambda p: ssend.at[p], lambda p: srecv.at[p], 2)
    for c in range(2, 4):
        relay(c)

    run[...] = jnp.zeros_like(run)
    eacc[...] = jnp.zeros_like(eacc)
    half_arrived(5)
    for s in range(S):
        wall[WR * s : WR * s + WR, :] = wrecv[s].astype(wall.dtype)
    wallb[...] = wall[...].astype(BF16)
    own.wait()

    lane64 = lax.broadcasted_iota(jnp.int32, (1, 64), 1)
    lane512 = lax.broadcasted_iota(jnp.int32, (1, HD * 128), 1)
    ones_col = lax.rem(lane512, 128) == HV

    def chunk(c, x):
        @pl.when(c == 2)
        def _():
            relay(4)

        @pl.when(c == 4)
        def _():
            relay(5)

        for way in (0, 1):
            onward(way, c).wait_recv()
        rows = pl.ds(pl.multiple_of(c * C, C), C)
        acc = jnp.zeros((C, 640), F32)
        for z in range(Z):
            acc = acc + dot(gat[z, rows, :], wallb[z * FW : (z + 1) * FW, :])
        qk32 = acc[:, :128]
        qk = qk32.astype(BF16)
        v = jnp.where(ones_col, 1.0, acc[:, 128:].astype(BF16).astype(F32))
        qkT = jnp.transpose(qk.astype(F32)).astype(BF16)
        pq = (dot(qk, q1[...]) * (dot(qk, q2[...]) + bq[1:2, :]) + bq[0:1, :]).astype(BF16)
        psiq[rows, :] = pq
        pk = (dot(k1[...], qkT) * (dot(k2[...], qkT) + bk[:, 1:2]) + bk[:, 0:1]).astype(BF16)
        pos_col = c * C + lax.broadcasted_iota(jnp.int32, (C, 1), 0)
        pos_row = c * C + lax.broadcasted_iota(jnp.int32, (1, C), 1)
        slot_col = slot_of(pos_col)
        slot_row = slot_of(pos_row)
        slot_top = jnp.int32(0)
        slot_next = jnp.int32(0)
        for stop in stops:
            slot_top = slot_top + (c * C >= stop).astype(jnp.int32)
            slot_next = slot_next + (c * C + C >= stop).astype(jnp.int32)
        allowed = (slot_col == slot_row) & (pos_row <= pos_col)
        from_top = (slot_col == slot_top).astype(F32)
        keep = (slot_top == slot_next).astype(F32)
        q64 = qk32[:, :64].astype(BF16).astype(F32)
        for h in range(HD):
            head = (lane64 >= 16 * h) & (lane64 < 16 * h + 16)
            a = dot(jnp.where(head, q64, 0.0).astype(BF16), qkT[64:, :]) * 0.25
            weight = jnp.where(allowed, 1.0 + a + 0.5 * a * a, 0.0).astype(BF16)
            vh = v[:, 128 * h : 128 * h + 128]
            state = run[h]
            s_hi = state.astype(BF16)
            s_lo = (state - s_hi.astype(F32)).astype(BF16)
            pqh = pq[:, 256 * h : 256 * h + 256]
            both = dot(pqh, jnp.concatenate([s_hi, s_lo], axis=1))
            num[rows, 128 * h : 128 * h + 128] = dot(weight, vh.astype(BF16)) + from_top * (
                both[:, :128] + both[:, 128:]
            )
            parts = []
            for j in range(ENDS):
                mark = (slot_col == j) & (stops[j] <= T)
                parts.append(jnp.where(mark, vh, 0.0).astype(BF16))
            parts.append(jnp.where(slot_col == slot_next, vh, 0.0).astype(BF16))
            made = dot(pk[256 * h : 256 * h + 256, :], jnp.concatenate(parts, axis=1))
            eacc[h] += made[:ROWS, : ENDS * 128]
            run[h] = keep * state + made[:, ENDS * 128 :]
        return x

    lax.fori_loop(0, NC, chunk, 0)

    for s in range(S):
        h, k = s // PH, s % PH
        rows = slice(SR * k, SR * k + SR)
        lsend[s, ENDS] = run[h, rows, :].astype(BF16)
        for j in range(ENDS):
            lsend[s, j] = eacc[h, rows, 128 * j : 128 * j + 128].astype(BF16)
    exchange(lambda p: lsend.at[p], lambda p: lrecv.at[p], 3)

    arrived(srecv, 2)
    for s in range(S):
        h, k = s // PH, s % PH
        for j in range(SLOTS):
            start[h, SR * k : SR * k + SR, 128 * j : 128 * j + 128] = srecv[s, j].astype(F32)
    start[:, ROWS:, :] = jnp.zeros((HD, 256 - ROWS, SLOTS * 128), F32)

    def begin(c, x):
        rows = pl.ds(pl.multiple_of(c * C, C), C)
        slot_col = slot_of(c * C + lax.broadcasted_iota(jnp.int32, (C, 1), 0))
        for h in range(HD):
            got = dot(psiq[rows, 256 * h : 256 * h + 256], start[h].astype(BF16))
            add = jnp.zeros((C, 128), F32)
            for j in range(SLOTS):
                add = jnp.where(slot_col == j, got[:, 128 * j : 128 * j + 128], add)
            num[rows, 128 * h : 128 * h + 128] += add
        return x

    lax.fori_loop(0, NC, begin, 0)

    arrived(lrecv, 3)

    def carry(b, c):
        csend[b, 0] = c.astype(BF16)
        go_on = (first[b] == first[b + 1]).astype(F32)
        ftab[b] = c
        return c * go_on + lrecv[b, ENDS].astype(F32)

    lax.fori_loop(0, S, carry, jnp.zeros((SR, 128), F32))

    def finish(o, x):
        r = inv[o]
        b = jnp.clip(lax.div(ends[r] - 1, T), 0, S - 1)
        j = jnp.clip(r - first[b], 0, ENDS - 1)
        lead = (j == 0).astype(F32)
        csend[o, 1] = (lrecv[b, j].astype(F32) + lead * ftab[b]).astype(BF16)
        return x

    lax.fori_loop(0, S, finish, 0)
    exchange(lambda p: csend.at[p], lambda p: crecv.at[p], 4)
    arrived(crecv, 4)
    for s in range(S):
        h, k = s // PH, s % PH
        rows = slice(SR * k, SR * k + SR)
        run[h, rows, :] = crecv[s, 0].astype(F32)
        stage[rows, 128 * h : 128 * h + 128] = crecv[s, 1].astype(F32)
    run[:, ROWS:, :] = jnp.zeros((HD, 256 - ROWS, 128), F32)

    def close(c, x):
        rows = pl.ds(pl.multiple_of(c * C, C), C)
        slot_col = slot_of(c * C + lax.broadcasted_iota(jnp.int32, (C, 1), 0))
        parts = []
        for h in range(HD):
            got = dot(psiq[rows, 256 * h : 256 * h + 256], run[h].astype(BF16))
            both = num[rows, 128 * h : 128 * h + 128] + jnp.where(slot_col == 0, got, 0.0)
            parts.append((both / both[:, HV : HV + 1]).astype(BF16))
        out[rows, :] = dot(jnp.concatenate(parts, axis=1), pack[...]).astype(BF16)
        return x

    lax.fori_loop(0, NC, close, 0)

    got = stage[...].astype(BF16)
    flag = resume[inv[me]].astype(F32)
    fstate[0] = flag * init[0] + spread_s[...] * dot(spread[...], dot(got, pack[...]).astype(BF16))
    moved = spread_t[...] * dot_nt(dot_nt(unpack_n[...], got).astype(BF16), spread[...])
    fnorm[0] = flag * norm[0] + moved

    for c in range(NC):
        for way in (0, 1):
            direct(way, c).wait_send()
            onward(way, c).wait_send()
    for n, buf in ((0, isend), (2, ssend), (3, lsend), (4, csend)):
        sent(buf, n)
    for n, copies in ((1, S // 2 - 1), (5, S // 2)):
        part = wrecv.at[pl.ds(0, copies)]
        pltpu.make_async_copy(part, part, xsend.at[n]).wait()


def local(tokens, wq, wk, wv, lengths, owner, resume, init, norm):
    S, Z = lax.axis_size("seq"), lax.axis_size("tp")
    norm = jnp.transpose(norm, (0, 2, 1))
    T, FW = tokens.shape
    C = T // 6
    SR = HD * ROWS // S
    consts = tables(float(T * S // 2))
    smem = pl.BlockSpec(memory_space=pltpu.SMEM)
    vmem = pl.BlockSpec(memory_space=pltpu.VMEM)
    hbm = pl.BlockSpec(memory_space=pl.ANY)
    out, state, moved = pl.pallas_call(
        functools.partial(kernel, S, Z, C),
        out_shape=(
            jax.ShapeDtypeStruct((T, HD * HV), BF16),
            jax.ShapeDtypeStruct(init.shape, F32),
            jax.ShapeDtypeStruct(norm.shape, F32),
        ),
        in_specs=[smem] * 3 + [hbm] + [vmem] * (5 + len(consts)),
        out_specs=(vmem, vmem, vmem),
        scratch_shapes=[
            pltpu.VMEM((Z, T, FW), BF16),
            pltpu.VMEM((wq.shape[0], 640), BF16),
            pltpu.VMEM((S, wq.shape[0], 640), BF16),
            pltpu.VMEM((S * wq.shape[0], 640), F32),
            pltpu.VMEM((S * wq.shape[0], 640), BF16),
            pltpu.VMEM((ROWS, HD * 128), F32),
            pltpu.VMEM((S, SR, 128), BF16),
            pltpu.VMEM((S, SR, 128), BF16),
            pltpu.VMEM((S, SLOTS, SR, 128), BF16),
            pltpu.VMEM((S, SLOTS, SR, 128), BF16),
            pltpu.VMEM((HD, 256, SLOTS * 128), F32),
            pltpu.VMEM((S, SLOTS, SR, 128), BF16),
            pltpu.VMEM((S, SLOTS, SR, 128), BF16),
            pltpu.VMEM((S, 2, SR, 128), BF16),
            pltpu.VMEM((S, 2, SR, 128), BF16),
            pltpu.VMEM((T, HD * 256), BF16),
            pltpu.VMEM((T, HD * 128), F32),
            pltpu.VMEM((HD, ROWS, ENDS * 128), F32),
            pltpu.VMEM((HD, 256, 128), F32),
            pltpu.VMEM((S, SR, 128), F32),
            pltpu.SMEM((S,), jnp.int32),
            pltpu.SMEM((S + 1,), jnp.int32),
            pltpu.SMEM((S,), jnp.int32),
            pltpu.SemaphoreType.DMA,
            pltpu.SemaphoreType.DMA((2, 6)),
            pltpu.SemaphoreType.DMA((2, 6)),
            pltpu.SemaphoreType.DMA((2, 6)),
            pltpu.SemaphoreType.DMA((2, 6)),
            pltpu.SemaphoreType.DMA((6,)),
            pltpu.SemaphoreType.DMA((6,)),
        ],
        compiler_params=pltpu.CompilerParams(
            collective_id=0, has_side_effects=True, vmem_limit_bytes=60 * 2**20
        ),
    )(lengths, owner, resume, tokens, wq, wk, wv, init, norm, *consts)
    return out, state, jnp.transpose(moved, (0, 2, 1))


def solution(mesh):
    in_specs = (
        P("seq", "tp"),
        P("seq", "tp"),
        P("seq", "tp"),
        P("seq", "tp"),
        P(),
        P(),
        P(),
        P("seq", None, "tp"),
        P("seq", None, "tp"),
    )
    out_specs = (P("seq", "tp"), P("seq", None, "tp"), P("seq", None, "tp"))
    return jax.shard_map(local, mesh=mesh, in_specs=in_specs, out_specs=out_specs, check_vma=False)
```
